32 devices in a mesh: dp: 4 (over y, x), inner: 8 (over z, core).
Axes of the slice: x: 2, y: 2, z: 4, core: 2. Of those that a mesh axis runs over, the one named last changes fastest.
Arguments:
- queries: bfloat16 [32, 32, 128], P(('dp', 'inner'))
- labels: int32 [32], P(('dp', 'inner')), may hold values from 0 to 127
- pages: bfloat16 [128, 1024, 128], P(('dp', 'inner'))
Outputs:
- grad_queries: float32 [32, 32, 128], P(('dp', 'inner'))
- grad_pages: float32 [128, 1024, 128], P(('dp', 'inner'))
The draws below stay inside these ranges and needn't reach their ends.
All inputs are finite; a program needn't handle non-finite values.
Results may differ from the reference program's by a relative error of at most 0.0029.
Values may be sent and summed in bfloat16 or wider, within the bound.
No kernel may reach another device: no remote copies, remote signals or barrier semaphores. Data moves between devices by JAX's collectives and lax.ppermute only.
A program may use at most 64 MiB of HBM per device.

```python
import jax
import jax.numpy as jnp
from jax import lax

D = 128
LQ = 32
LP = 1024
QUERIES = 32
PAGES = 128


def draw_pages(key, part):
    values = jax.random.normal(jax.random.fold_in(key, 11), (PAGES, LP, D), jnp.float32) * D ** (-0.25)
    return values.astype(jnp.bfloat16)


def draw_queries(key, part):
    values = jax.random.normal(jax.random.fold_in(key, 12), (QUERIES, LQ, D), jnp.float32) * D ** (-0.25)
    return values.astype(jnp.bfloat16)


def place_ends(result, own_key, low, high):
    index_at = [jax.random.randint(jax.random.fold_in(own_key, axis), (), 0, length) for axis, length in enumerate(result.shape)]
    longest = result.shape.index(max(result.shape))
    next_to = index_at[:longest] + [(index_at[longest] + 1) % result.shape[longest]] + index_at[longest + 1:]
    return result.at[tuple(index_at)].set(low).at[tuple(next_to)].set(high)


def setup_inputs(seed: int = 0) -> dict:
    seeds = jax.random.split(jax.random.key(seed), 4)
    return {
        "queries": draw_queries(jax.random.fold_in(seeds[3], 71), 0),
        "labels": place_ends(jax.random.randint(seeds[1], (QUERIES,), 0, PAGES), jax.random.fold_in(seeds[1], 1), 0, PAGES - 1).astype(jnp.int32),
        "pages": draw_pages(jax.random.fold_in(seeds[3], 71), 0),
    }


def reference(queries, labels, pages):
    flat_rows = queries.reshape(QUERIES * LQ, D)

    def visit(query_grad, inputs):
        page_block, page_number = inputs
        scores = jnp.dot(flat_rows, page_block.T, preferred_element_type=jnp.float32)
        weights = jax.nn.softmax(scores, axis=-1)
        matched = jnp.sum(weights * scores, axis=-1)
        summed = matched.reshape(QUERIES, LQ).sum(axis=1)
        signs = jnp.where(labels == page_number, jnp.float32(1.0), jnp.float32(-1.0))
        logits = summed - jnp.float32(LQ)
        grad_score = -signs * jax.nn.sigmoid(-signs * logits)
        row_grad = jnp.broadcast_to(grad_score[:, None], (QUERIES, LQ)).reshape(QUERIES * LQ)
        dscore = (row_grad[:, None] * weights * (1.0 + scores - matched[:, None])).astype(jnp.bfloat16)
        query_grad = query_grad + jnp.dot(dscore, page_block, preferred_element_type=jnp.float32)
        page_grad = jnp.dot(dscore.T, flat_rows, preferred_element_type=jnp.float32)
        return query_grad, page_grad

    start_grad = jnp.zeros((QUERIES * LQ, D), jnp.float32)
    numbers = jnp.arange(PAGES, dtype=jnp.int32)
    query_grad, page_grads = lax.scan(visit, start_grad, (pages, numbers))
    return query_grad.reshape(QUERIES, LQ, D), page_grads
```

```python
import functools, math
import jax, jax.numpy as jnp
from jax import lax
from jax.experimental import pallas as pl
from jax.experimental.pallas import tpu as pltpu
from jax.sharding import PartitionSpec as P

LOG2E = math.log2(math.e)
LN2 = math.log(2.0)
F32, BF16 = jnp.float32, jnp.bfloat16


def dot(a, b, ca, cb):
    return lax.dot_general(a, b, (((ca,), (cb,)), ((), ())), preferred_element_type=F32)


def split3(x):
    hi = x.astype(BF16)
    r = x - hi.astype(F32)
    mid = r.astype(BF16)
    lo = (r - mid.astype(F32)).astype(BF16)
    return hi, mid, lo


def kernel(tq, tokens, ch, first_ref, qx_ref, pages_ref, gq_ref, gp_hbm,
           qhl, lab, pt, st0, et0, et1, ft0, ft1, mx, stat0, stat1, cs0, cs1, qs0, qs1, gqt, gp, sem):
    npages, lp, d = pages_ref.shape
    nt = qx_ref.shape[0] // tq
    rows = tq * tokens
    n = npages * nt
    nch = lp // ch

    lane_q = lax.broadcasted_iota(jnp.int32, (rows, rows), 1) // tokens
    sub_q = lax.broadcasted_iota(jnp.int32, (rows, rows), 0) // tokens
    seg = (lane_q == sub_q).astype(BF16)

    def setup(t, _):
        blk = qx_ref[pl.ds(t * tq, tq)]
        q = blk[:, :tokens, :].reshape(rows, d)
        qs = q.astype(F32) * LOG2E
        hi = qs.astype(BF16)
        lo = (qs - hi.astype(F32)).astype(BF16)
        qhl[t, :, :d] = hi
        qhl[t, :, d:] = lo
        lrow = blk[:, tokens:tokens + 1, :].reshape(tq, d)
        lane = lax.broadcasted_iota(jnp.int32, (tq, rows), 1) // tokens
        sub = lax.broadcasted_iota(jnp.int32, (tq, rows), 0)
        onehot = (lane == sub).astype(BF16)
        digits = dot(lrow, onehot, 0, 0)
        lab[t] = digits[:8]
        gqt[t] = jnp.zeros((d, rows), F32)
        return 0

    lax.fori_loop(0, nt, setup, 0)

    def setup_p(p, _):
        pt[p] = pages_ref[p].T
        return 0

    lax.fori_loop(0, npages, setup_p, 0)

    def a1(i, c, st):
        p, t = i // nt, i % nt
        q2 = qhl[t]
        sl = slice(c * ch, (c + 1) * ch)
        pc = pages_ref[p, sl, :]
        s = dot(jnp.concatenate([pc, pc], axis=1), q2, 1, 1)
        st[sl, :] = s
        return jnp.max(s.reshape(ch // 8, 8, rows), axis=0)

    def a2(c, m, st, et, ft):
        sl = slice(c * ch, (c + 1) * ch)
        tt = st[sl, :] - m
        e = jnp.exp2(tt)
        f = e * tt
        et[sl, :] = e
        ft[sl, :] = f
        return jnp.sum(e.reshape(ch // 8, 8, rows), axis=0), jnp.sum(f.reshape(ch // 8, 8, rows), axis=0)

    def b0(i, stat):
        p, t = i // nt, i % nt
        m, l, f = stat[0:1], stat[1:2], stat[2:3]
        inv = 1.0 / l
        mm = f * inv
        matched = (mm + m) * LN2
        hi, mid, lo = split3(matched)
        parts = jnp.concatenate([hi.astype(F32), mid.astype(F32), lo.astype(F32), jnp.zeros((5, rows), F32)], axis=0)
        sums = dot(parts.astype(BF16), seg, 1, 0)
        score = sums[0:1] + sums[1:2] + sums[2:3]
        digits = lab[t]
        label = digits[0:1].astype(jnp.int32) * 256 + digits[1:2].astype(jnp.int32)
        sign = jnp.where(label == first_ref[0] + p, 1.0, -1.0).astype(F32)
        logit = score - float(tokens)
        g = -sign * jax.nn.sigmoid(-sign * logit)
        c2 = g * (inv * LN2)
        c1 = LOG2E - mm
        c2col = jnp.broadcast_to(c2, (d, rows)).T
        q = qx_ref[pl.ds(t * tq, tq)][:, :tokens, :].reshape(rows, d)
        qs = (q.astype(F32) * c2col).astype(BF16)
        return c1, c2, qs

    def b1(i, c, c1, qsr, et, ft):
        p = i // nt
        sl = slice(c * ch, (c + 1) * ch)
        ds = (ft[sl, :] + c1 * et[sl, :]).astype(BF16)
        gp[p, sl, :] = gp[p, sl, :] + dot(ds, qsr[...], 1, 0)
        return dot(pt[p, :, sl], ds, 1, 0)

    ets, fts, stats, cs, qss = (et0, et1), (ft0, ft1), (stat0, stat1), (cs0, cs1), (qs0, qs1)

    def step(k, par, w1, w2, w3, w4):
        et, ft = ets[par], fts[par]
        if w4:
            c1, c2 = cs[par][0:1], cs[par][1:2]
        if w2:
            m = jnp.max(mx[...], axis=0, keepdims=True)
        l8 = f8 = m8 = acc = None
        for c in range(nch):
            if w4:
                x = b1(k, c, c1, qss[par], et, ft)
                acc = x if acc is None else acc + x
            if w2:
                le, fe = a2(c, m, st0, et, ft)
                l8, f8 = (le, fe) if l8 is None else (l8 + le, f8 + fe)
            if w1:
                x = a1(k + 3, c, st0)
                m8 = x if m8 is None else jnp.maximum(m8, x)
            if c == 0 and w3:
                c1n, c2n, qsn = b0(k + 1, stats[1 - par])
                cs[1 - par][0:1] = c1n
                cs[1 - par][1:2] = c2n
                qss[1 - par][...] = qsn
        if w1:
            mx[...] = m8
        if w2:
            stats[par][0:1] = m
            stats[par][1:2] = jnp.sum(l8, axis=0, keepdims=True)
            stats[par][2:3] = jnp.sum(f8, axis=0, keepdims=True)
        if w4:
            p, t = k // nt, k % nt
            gqt[t] = gqt[t] + acc * c2
            @pl.when(t == nt - 1)
            def _():
                pltpu.make_async_copy(gp.at[p], gp_hbm.at[p], sem).start()

    for p in range(npages):
        gp[p] = jnp.zeros((lp, d), F32)

    assert n % 2 == 0 and n >= 4
    step(-3, 1, 1, 0, 0, 0)
    step(-2, 0, 1, 1, 0, 0)
    step(-1, 1, 1, 1, 1, 0)

    def body(k, _):
        step(2 * k, 0, 1, 1, 1, 1)
        step(2 * k + 1, 1, 1, 1, 1, 1)
        return 0

    lax.fori_loop(0, n // 2 - 2, body, 0)
    step(n - 4, 0, 1, 1, 1, 1)
    step(n - 3, 1, 0, 1, 1, 1)
    step(n - 2, 0, 0, 0, 1, 1)
    step(n - 1, 1, 0, 0, 0, 1)

    def fin(t, _):
        gq_ref[pl.ds(t * tq, tq)] = gqt[t].T.astype(gq_ref.dtype).reshape(tq, tokens, d)
        return 0
    lax.fori_loop(0, nt, fin, 0)
    for p in range(npages):
        pltpu.make_async_copy(gp.at[p], gp_hbm.at[p], sem).wait()


def call(first, qx, pages, tokens, tq=8, ch=256):
    nq = qx.shape[0]
    npages, lp, d = pages.shape
    rows = tq * tokens
    nt = nq // tq
    return pl.pallas_call(
        functools.partial(kernel, tq, tokens, ch),
        out_shape=(jax.ShapeDtypeStruct((nq, tokens, d), BF16), jax.ShapeDtypeStruct((npages, lp, d), F32)),
        in_specs=[pl.BlockSpec(memory_space=pltpu.SMEM), pl.BlockSpec(memory_space=pltpu.VMEM), pl.BlockSpec(memory_space=pltpu.VMEM)],
        out_specs=(pl.BlockSpec(memory_space=pltpu.VMEM), pl.BlockSpec(memory_space=pl.ANY)),
        scratch_shapes=[
            pltpu.VMEM((nt, rows, 2 * d), BF16),
            pltpu.VMEM((nt, 8, rows), F32),
            pltpu.VMEM((npages, d, lp), BF16),
            pltpu.VMEM((lp, rows), F32),
            pltpu.VMEM((lp, rows), F32),
            pltpu.VMEM((lp, rows), F32),
            pltpu.VMEM((lp, rows), F32),
            pltpu.VMEM((lp, rows), F32),
            pltpu.VMEM((8, rows), F32),
            pltpu.VMEM((8, rows), F32),
            pltpu.VMEM((8, rows), F32),
            pltpu.VMEM((8, rows), F32),
            pltpu.VMEM((8, rows), F32),
            pltpu.VMEM((rows, d), BF16),
            pltpu.VMEM((rows, d), BF16),
            pltpu.VMEM((nt, d, rows), F32),
            pltpu.VMEM((npages, lp, d), F32),
            pltpu.SemaphoreType.DMA,
        ],
        compiler_params=pltpu.CompilerParams(vmem_limit_bytes=40 * 2**20),
        name="pairs",
    )(first, qx, pages)


def shards(queries, labels, pages):
    count, tokens, width = queries.shape
    axes = ("dp", "inner")
    devices = lax.axis_size("dp") * lax.axis_size("inner")
    first = (lax.axis_index(axes) * pages.shape[0]).astype(jnp.int32).reshape(1)
    lane = lax.broadcasted_iota(jnp.int32, (count, 8, width), 2)
    digits = jnp.where(lane == 0, labels[:, None, None] // 256, labels[:, None, None] % 256)
    packed = jnp.concatenate([queries, digits.astype(BF16)], axis=1)
    spread = jnp.broadcast_to(packed[None], (devices,) + packed.shape)
    every = lax.all_to_all(spread, axes, 0, 0, tiled=True).reshape((devices * count,) + packed.shape[1:])
    partial, page_grads = call(first, every, pages, tokens)
    mine = lax.all_to_all(partial.reshape(devices, count, tokens, width), axes, 0, 0, tiled=True)
    return jnp.sum(mine.astype(F32), axis=0), page_grads


def solution(mesh):
    placed = (P(("dp", "inner"), None, None), P(("dp", "inner")), P(("dp", "inner"), None, None))
    return jax.shard_map(
        shards,
        mesh=mesh,
        in_specs=placed,
        out_specs=(P(("dp", "inner"), None, None), P(("dp", "inner"), None, None)),
        check_vma=False,
    )
```
